32 devices in a mesh: gx: 8 (over y, x, core), gy: 4 (over z).
Axes of the slice: x: 2, y: 2, z: 4, core: 2. Of those that a mesh axis runs over, the one named last changes fastest.
Arguments:
- activations: bfloat16 [1024, 7168], P('gx', 'gy'), may hold values from -6 to 6
- out_grad: bfloat16 [1024, 7168], P('gx', 'gy'), may hold values from -0.59765625 to 0.59765625
- saved_gate: bfloat16 [1024, 2, 1024], P('gx', None, 'gy'), may hold values from -9 to 9
- saved_up: bfloat16 [1024, 2, 1024], P('gx', None, 'gy'), may hold values from -6 to 6
- route_ids: int32 [1024, 2], P('gx'), may hold values from 0 to 7, all different within a row; in each aligned block of 128 rows (0 to 127, 128 to 255, ...) at most 48 rows name the same one
- route_weight: float32 [1024, 2], P('gx'), may hold values from 0.1 to 1
- down_weight: bfloat16 [8, 1024, 7168], P('gx', None, 'gy'), may hold values from -0.1875 to 0.1875
Outputs:
- grad_gate: bfloat16 [8, 7168, 1024], P('gx', 'gy')
- grad_up: bfloat16 [8, 7168, 1024], P('gx', 'gy')
- grad_down: bfloat16 [8, 1024, 7168], P('gx', None, 'gy')
The draws below stay inside these ranges and needn't reach their ends.
Inputs may be any that keep to these rules, and one draw needn't show every extreme that they name: `route_ids`: each token names 2 different experts. Within each aligned block of 128 tokens (one index of gx) no expert is named by more than 48 tokens, a bound that some block reaches.
All inputs are finite; a program needn't handle non-finite values.
Results may differ from the reference program's by a relative error of at most 0.02.
Values may be sent and summed in bfloat16 or wider, within the bound.
A program may use at most 64 MiB of HBM per device.

```python
import math
import jax
import jax.numpy as jnp
import numpy as np
from jax import lax

D = 7168
HIDDEN_SIZE = 1024
TOK_DEV = 128
TOP = 2
MOST = 48
EXPERTS = 8
TOKENS = 1024
ROWS = 384
N_GX = 8
N_GY = 4


def level_of(key, shape, pieces, smallest, high):
    level, own = 1.0, jax.random.fold_in(key, 6)
    for position, blocks in pieces:
        heights = jnp.exp(jax.random.uniform(jax.random.fold_in(own, position), (blocks,), jnp.float32, smallest / len(pieces), high / len(pieces)))
        level = level * jnp.repeat(heights, shape[position] // blocks).reshape([-1 if axis == position else 1 for axis in range(len(shape))])
    return level


def assign_block(key, own, number, rows, number_of, top, most, lean):
    ranking = jax.random.permutation(key, number_of)
    crowded, ordinary = portions_of(number_of, rows * top, most, lean, True), portions_of(number_of, rows * top, most, lean, False)
    places = jnp.arange(number_of)

    def named(tallies, rotation):
        used = int((tallies > 0).sum())
        fixed = max(1, used // 4)
        moved = fixed + (places - fixed + rotation * (used - fixed)) % max(1, number_of - fixed)
        return jnp.zeros((number_of,), jnp.int32).at[ranking[jnp.where(places < fixed, places, moved)]].set(jnp.asarray(tallies, jnp.int32))

    tallies = jnp.where(number % 4 == 0, named(crowded, number // 4), named(ordinary, number - number // 4 - 1))
    mixed = jax.random.permutation(jax.random.fold_in(own, 3), number_of)
    donor, sink = mixed[0:number_of // 2 * 2:2], mixed[1:number_of // 2 * 2:2]
    slack = jnp.minimum(tallies[donor] - 1, most - tallies[sink]) // 2
    slack = jnp.where((donor == ranking[0]) | (sink == ranking[0]) | (tallies[sink] == 0), 0, jnp.maximum(slack, 0))
    moved = jax.random.randint(jax.random.fold_in(own, 4), (number_of // 2,), 0, 1 << 20) % (slack + 1)
    tallies = tallies.at[donor].add(-moved).at[sink].add(moved)
    items = jnp.searchsorted(jnp.cumsum(tallies), jnp.arange(rows * top), side="right").astype(jnp.int32)
    grid = items.reshape(top, rows).T
    grid = grid[jax.random.permutation(jax.random.fold_in(own, 1), rows)]
    rotation = jax.random.randint(jax.random.fold_in(own, 2), (rows, 1), 0, top)
    return jnp.take_along_axis(grid, (jnp.arange(top)[None, :] + rotation) % top, axis=1)


def portions_of(number_of, total, limit, skew, full):
    loads = [(1 << 20) // math.isqrt(standing ** skew) + 1 for standing in range(1, number_of + 1)]
    largest = limit if full else min(limit, max(-(-total // number_of), total * loads[0] // sum(loads)))
    least = 1 if total - largest >= number_of - 1 else 0
    holding, rest = [largest] + [least] * (number_of - 1), total - largest - least * (number_of - 1)
    while rest > 0:
        candidates = [i for i in range(1, number_of) if holding[i] < largest] or [i for i in range(1, number_of) if holding[i] < limit]
        whole, left = sum([loads[i] for i in candidates]), rest
        for i in candidates:
            extra = min(limit - holding[i], max(1, left * loads[i] // whole), rest)
            holding[i] = holding[i] + extra
            rest = rest - extra
    return np.array(holding)


def normal_values(rng, shape, spread, bound, pieces=(), kind=jnp.bfloat16):
    values = spread * jax.random.normal(rng, shape, jnp.float32)
    if pieces:
        values = values * level_of(rng, shape, pieces, -0.22, 0.18)
    return jnp.clip(values, -bound, bound).astype(kind)


def setup_inputs(seed: int = 0) -> dict:
    streams_of = jax.random.split(jax.random.key(seed), 8)
    activations = normal_values(streams_of[0], (TOKENS, D), 1.0, 6.0, ((0, 8), (1, 4)))
    out_grad = normal_values(streams_of[1], (TOKENS, D), 0.1, 0.59765625, ((0, 8), (1, 4)))
    saved_gate = normal_values(streams_of[2], (TOKENS, TOP, HIDDEN_SIZE), 1.5, 9.0, ((0, 8), (2, 4)))
    saved_up = normal_values(streams_of[3], (TOKENS, TOP, HIDDEN_SIZE), 1.0, 6.0, ((0, 8), (2, 4)))
    route_ids_keys = jax.random.split(jax.random.fold_in(streams_of[4], 1), TOKENS // TOK_DEV)
    route_ids_turns = jax.random.permutation(jax.random.fold_in(streams_of[4], 3), TOKENS // TOK_DEV)
    route_ids = jax.vmap(lambda own, number: assign_block(jax.random.fold_in(streams_of[4], 2), own, number, TOK_DEV, EXPERTS, TOP, MOST, 2))(route_ids_keys, route_ids_turns).reshape((TOKENS, TOP))
    route_weight = jnp.clip(jnp.exp(math.log(1.0) - 2.3025851 * jax.random.uniform(streams_of[5], (TOKENS, TOP), jnp.float32) ** level_of(streams_of[5], (TOKENS, TOP), ((0, 8),), -0.2, 0.2)), 0.1, 1.0)
    down_weight = normal_values(streams_of[6], (EXPERTS, HIDDEN_SIZE, D), HIDDEN_SIZE ** -0.5, 0.1875, ((0, 8), (2, 4)))
    return {"activations": activations, "out_grad": out_grad, "saved_gate": saved_gate, "saved_up": saved_up, "route_ids": route_ids, "route_weight": route_weight, "down_weight": down_weight}


def local_grads(hidden_grad, gate_rows, up_rows):
    gate_val = gate_rows.astype(jnp.float32)
    up_val = up_rows.astype(jnp.float32)
    gate_sig = jax.nn.sigmoid(gate_val)
    silu_val = gate_val * gate_sig
    hidden_act = (silu_val * up_val).astype(jnp.bfloat16)
    grad_upper = (hidden_grad * silu_val).astype(jnp.bfloat16)
    grad_gated = (hidden_grad * up_val * gate_sig * (1.0 + gate_val * (1.0 - gate_sig))).astype(jnp.bfloat16)
    return hidden_act, grad_gated, grad_upper


def contract_rows(left, right):
    return lax.dot_general(left, right, (((0,), (0,)), ((), ())), preferred_element_type=jnp.float32).astype(jnp.bfloat16)


def reference(activations, out_grad, saved_gate, saved_up, route_ids, route_weight, down_weight):
    routes_all = TOKENS * TOP
    block_ids = route_ids.reshape(N_GX, TOK_DEV * TOP)
    onehot = (block_ids[:, :, None] == jnp.arange(EXPERTS, dtype=jnp.int32)[None, None, :]).astype(jnp.int32)
    rank_in = jnp.sum((jnp.cumsum(onehot, axis=1) - onehot) * onehot, axis=2).reshape(-1).astype(jnp.int32)
    source = (jnp.arange(routes_all, dtype=jnp.int32) // (TOK_DEV * TOP)).astype(jnp.int32)
    flat_ids = route_ids.reshape(-1).astype(jnp.int32)
    destination = (flat_ids * ROWS + source * MOST + rank_in).astype(jnp.int32)
    numbers = jnp.arange(routes_all, dtype=jnp.int32) + 1
    row_table = jnp.zeros((EXPERTS * ROWS,), jnp.int32).at[destination].set(numbers).reshape(EXPERTS, ROWS)
    flat_weight = route_weight.reshape(-1)
    gate_flat = saved_gate.reshape(routes_all, HIDDEN_SIZE)
    up_flat = saved_up.reshape(routes_all, HIDDEN_SIZE)
    nothing = jnp.zeros((), jnp.bfloat16)

    def one_expert(packed):
        entry, weight = packed
        is_live = (entry > 0)[:, None]
        route_at = jnp.maximum(entry - 1, 0).astype(jnp.int32)
        token_at = (route_at // TOP).astype(jnp.int32)
        rows_act = jnp.where(is_live, activations[token_at], nothing)
        scaled = (flat_weight[route_at][:, None] * out_grad[token_at].astype(jnp.float32)).astype(jnp.bfloat16)
        rows_grad = jnp.where(is_live, scaled, nothing)
        gate_rows = jnp.where(is_live, gate_flat[route_at], nothing)
        up_rows = jnp.where(is_live, up_flat[route_at], nothing)
        split_grad = rows_grad.reshape(ROWS, N_GY, D // N_GY).astype(jnp.float32)
        split_weight = weight.reshape(HIDDEN_SIZE, N_GY, D // N_GY).astype(jnp.float32)
        partial_value = jnp.einsum("rgd,fgd->grf", split_grad, split_weight).astype(jnp.bfloat16)
        partial_value = lax.optimization_barrier(partial_value)
        hidden_grad = jnp.sum(partial_value.astype(jnp.float32), axis=0)
        hidden_act, grad_gated, grad_upper = local_grads(hidden_grad, gate_rows, up_rows)
        return contract_rows(rows_act, grad_gated), contract_rows(rows_act, grad_upper), contract_rows(hidden_act, rows_grad)

    grad_gate, grad_up, grad_down = lax.map(one_expert, (row_table, down_weight))
    return grad_gate, grad_up, grad_down
```

```python
import functools

import jax
import jax.numpy as jnp
from jax import lax
from jax.experimental import pallas as pl
from jax.experimental.pallas import tpu as pltpu
from jax.sharding import PartitionSpec as P

MOST = 48
F32 = jnp.float32
BF16 = jnp.bfloat16
MESH = pl.DeviceIdType.MESH


def contract_rows(left, right):
    return lax.dot_general(
        left, right, (((0,), (0,)), ((), ())), preferred_element_type=jnp.float32
    ).astype(jnp.bfloat16)


def dot(left, right):
    return jnp.dot(left, right, preferred_element_type=F32)


def exchange_kernel(
    n_gx,
    n_gy,
    top,
    act_ref,
    grad_ref,
    pre_ref,
    ids_ref,
    wt_ref,
    down_hbm,
    rows_act,
    rows_grad,
    ha_ref,
    gg_ref,
    gu_ref,
    down,
    act_send,
    grad_send,
    pre_all,
    pre_send,
    pre_rows,
    part,
    part_in,
    hid,
    fac_gate,
    fac_up,
    down_sem,
    act_ss,
    act_rs,
    grad_ss,
    grad_rs,
    all_ss,
    all_rs,
    pre_ss,
    pre_rs,
    part_ss,
    part_rs,
    hid_ss,
    hid_rs,
):
    me = lax.axis_index("gx")
    my = lax.axis_index("gy")
    tokens = act_ref.shape[0]
    routes = tokens * top
    slots = n_gx * MOST
    per = n_gx // n_gy
    block = per * MOST
    share = pre_ref.shape[1] // 2

    def to_gx(src, dst, ss, rs, other):
        return pltpu.make_async_remote_copy(
            src_ref=src, dst_ref=dst, send_sem=ss, recv_sem=rs,
            device_id={"gx": other}, device_id_type=MESH,
        )

    def to_gy(src, dst, ss, rs, other):
        return pltpu.make_async_remote_copy(
            src_ref=src, dst_ref=dst, send_sem=ss, recv_sem=rs,
            device_id={"gy": other}, device_id_type=MESH,
        )

    barrier = pltpu.get_barrier_semaphore()
    for d in range(1, n_gx):
        pl.semaphore_signal(
            barrier, inc=1, device_id={"gx": lax.rem(me + d, n_gx)}, device_id_type=MESH
        )
    for d in range(1, n_gy):
        pl.semaphore_signal(
            barrier, inc=1, device_id={"gy": lax.rem(my + d, n_gy)}, device_id_type=MESH
        )
    down_copy = pltpu.make_async_copy(down_hbm, down, down_sem)
    down_copy.start()
    pl.semaphore_wait(barrier, n_gx - 1 + n_gy - 1)

    for d in range(1, n_gy):
        other = lax.rem(my + d, n_gy)
        to_gy(pre_ref, pre_all.at[my], all_ss.at[d], all_rs.at[my], other).start()
    pre_all[my] = pre_ref[...]

    ids = ids_ref[...]
    height = max(n_gx, 16)
    expert = lax.broadcasted_iota(jnp.int32, (height, routes), 0)
    named = (expert == ids).astype(F32)
    before = lax.broadcasted_iota(jnp.int32, (tokens, tokens), 0)
    after = lax.broadcasted_iota(jnp.int32, (tokens, tokens), 1)
    less = (before < after).astype(F32).astype(BF16)
    upto = (before <= after).astype(F32).astype(BF16)
    named_low = named.astype(BF16)
    counts = []
    for kb in range(top):
        total = jnp.zeros((height, tokens), F32)
        for ka in range(top):
            total += dot(
                named_low[:, ka * tokens : (ka + 1) * tokens], upto if ka < kb else less
            )
        counts.append(total)
    count = jnp.concatenate(counts, axis=1)
    rank = jnp.sum(count * named, axis=0, keepdims=True)
    slot = ids * MOST + rank.astype(jnp.int32)
    places = lax.broadcasted_iota(jnp.int32, (slots, routes), 0)
    chosen = places == slot
    pick = chosen.astype(F32)
    weight = jnp.sum(pick * wt_ref[...], axis=1, keepdims=True)
    pick_tok = pick[:, :tokens]
    for k in range(1, top):
        pick_tok = pick_tok + pick[:, k * tokens : (k + 1) * tokens]
    pick_tok = pick_tok.astype(BF16)
    pick = pick.astype(BF16)

    width = grad_ref.shape[1]
    grad_send[...] = (
        (dot(pick_tok, grad_ref[...]) * weight).astype(BF16).reshape(n_gx, MOST, width)
    )
    for d in range(1, n_gx):
        other = lax.rem(me + d, n_gx)
        to_gx(
            grad_send.at[other], rows_grad.at[me], grad_ss.at[d], grad_rs.at[me], other
        ).start()
    rows_grad[me] = grad_send[me]

    act_send[...] = dot(pick_tok, act_ref[...]).astype(BF16).reshape(n_gx, MOST, width)
    for d in range(1, n_gx):
        other = lax.rem(me + d, n_gx)
        to_gx(
            act_send.at[other], rows_act.at[me], act_ss.at[d], act_rs.at[me], other
        ).start()
    rows_act[me] = act_send[me]

    down_copy.wait()
    home = me // per
    for i in range(n_gy):
        q = lax.rem(home + n_gy - i, n_gy)
        for j in range(per):
            s = q * per + j

            @pl.when(s != me)
            def _():
                to_gx(
                    grad_send.at[0], rows_grad.at[s], grad_ss.at[0], grad_rs.at[s], me
                ).wait_recv()

        rows = rows_grad[pl.ds(q * per, per)].reshape(block, width)
        value = lax.dot_general(
            rows, down[...], (((1,), (1,)), ((), ())), preferred_element_type=F32
        ).astype(BF16)
        part[q] = value

        @pl.when(q != my)
        def _():
            to_gy(part.at[q], part_in.at[my], part_ss.at[q], part_rs.at[my], q).start()

        @pl.when(q == my)
        def _():
            part_in[my] = part[q]

    for d in range(1, n_gy):
        other = lax.rem(my + d, n_gy)
        to_gy(pre_ref, pre_all.at[other], all_ss.at[0], all_rs.at[other], my).wait_recv()
    for y in range(n_gy):
        pre_send[:, y] = (
            dot(pick, pre_all[y]).astype(BF16).reshape(n_gx, MOST, 2 * share)
        )
    for d in range(1, n_gx):
        other = lax.rem(me + d, n_gx)
        to_gx(
            pre_send.at[other], pre_rows.at[me], pre_ss.at[d], pre_rs.at[me], other
        ).start()
    pre_rows[me] = pre_send[me]

    for d in range(1, n_gy):
        other = lax.rem(my + d, n_gy)
        to_gy(part.at[0], part_in.at[other], part_ss.at[0], part_rs.at[other], my).wait_recv()
    total = part_in[0].astype(F32)
    for y in range(1, n_gy):
        total = total + part_in[y].astype(F32)
    hid[my] = total.astype(BF16)
    for d in range(1, n_gy):
        other = lax.rem(my + d, n_gy)
        to_gy(hid.at[my], hid.at[my], hid_ss.at[d], hid_rs.at[my], other).start()

    for d in range(1, n_gx):
        other = lax.rem(me + d, n_gx)
        to_gx(pre_send.at[0], pre_rows.at[other], pre_ss.at[0], pre_rs.at[other], me).wait_recv()
    for q in range(n_gy):
        for y in range(n_gy):
            both = pre_rows[q * per : (q + 1) * per, y].reshape(block, 2 * share).astype(F32)
            gate, up = both[:, :share], both[:, share:]
            sig = jax.nn.sigmoid(gate)
            silu = gate * sig
            cols = slice(y * share, (y + 1) * share)
            ha_ref[q, :, cols] = (silu * up).astype(BF16)
            fac_up[q, :, cols] = silu
            fac_gate[q, :, cols] = up * sig * (1.0 + gate * (1.0 - sig))

    for d in range(1, n_gy):
        other = lax.rem(my + d, n_gy)
        to_gy(hid.at[0], hid.at[other], hid_ss.at[0], hid_rs.at[other], my).wait_recv()
    for q in range(n_gy):
        value = hid[q].astype(F32)
        gg_ref[q] = (value * fac_gate[q]).astype(BF16)
        gu_ref[q] = (value * fac_up[q]).astype(BF16)

    for d in range(1, n_gx):
        other = lax.rem(me + d, n_gx)
        to_gx(act_send.at[0], rows_act.at[other], act_ss.at[0], act_rs.at[other], me).wait_recv()
    for d in range(1, n_gx):
        other = lax.rem(me + d, n_gx)
        for src, dst, ss, rs in (
            (grad_send, rows_grad, grad_ss, grad_rs),
            (act_send, rows_act, act_ss, act_rs),
            (pre_send, pre_rows, pre_ss, pre_rs),
        ):
            to_gx(src.at[other], dst.at[me], ss.at[d], rs.at[me], other).wait_send()
    for d in range(1, n_gy):
        other = lax.rem(my + d, n_gy)
        to_gy(pre_ref, pre_all.at[my], all_ss.at[d], all_rs.at[my], other).wait_send()
        to_gy(part.at[other], part_in.at[my], part_ss.at[other], part_rs.at[my], other).wait_send()
        to_gy(hid.at[my], hid.at[my], hid_ss.at[d], hid_rs.at[my], other).wait_send()


def on_device(activations, out_grad, saved_gate, saved_up, route_ids, route_weight, down_weight):
    n_gx, n_gy = lax.axis_size("gx"), lax.axis_size("gy")
    tokens, top = route_ids.shape
    routes, slots = tokens * top, n_gx * MOST
    width, share = activations.shape[1], saved_gate.shape[2]
    hidden = down_weight.shape[1]
    rows = slots // n_gy
    ids = route_ids.T.reshape(1, routes)
    wt = route_weight.T.reshape(1, routes)
    pre = jnp.concatenate([saved_gate, saved_up], axis=2)
    pre = pre.transpose(1, 0, 2).reshape(routes, 2 * share)
    vmem = pl.BlockSpec(memory_space=pltpu.VMEM)
    dma = pltpu.SemaphoreType.DMA
    shape = jax.ShapeDtypeStruct
    rows_act, rows_grad, ha, gg, gu = pl.pallas_call(
        functools.partial(exchange_kernel, n_gx, n_gy, top),
        out_shape=(
            shape((n_gx, MOST, width), BF16),
            shape((n_gx, MOST, width), BF16),
            shape((n_gy, rows, hidden), BF16),
            shape((n_gy, rows, hidden), BF16),
            shape((n_gy, rows, hidden), BF16),
        ),
        in_specs=[vmem] * 5 + [pl.BlockSpec(memory_space=pl.ANY)],
        out_specs=[vmem] * 5,
        scratch_shapes=[
            pltpu.VMEM((hidden, width), BF16),
            pltpu.VMEM((n_gx, MOST, width), BF16),
            pltpu.VMEM((n_gx, MOST, width), BF16),
            pltpu.VMEM((n_gy, routes, 2 * share), BF16),
            pltpu.VMEM((n_gx, n_gy, MOST, 2 * share), BF16),
            pltpu.VMEM((n_gx, n_gy, MOST, 2 * share), BF16),
            pltpu.VMEM((n_gy, rows, hidden), BF16),
            pltpu.VMEM((n_gy, rows, hidden), BF16),
            pltpu.VMEM((n_gy, rows, hidden), BF16),
            pltpu.VMEM((n_gy, rows, hidden), F32),
            pltpu.VMEM((n_gy, rows, hidden), F32),
            dma,
            dma((n_gx,)), dma((n_gx,)), dma((n_gx,)), dma((n_gx,)),
            dma((n_gy,)), dma((n_gy,)),
            dma((n_gx,)), dma((n_gx,)),
            dma((n_gy,)), dma((n_gy,)), dma((n_gy,)), dma((n_gy,)),
        ],
        compiler_params=pltpu.CompilerParams(
            collective_id=0, has_side_effects=True, vmem_limit_bytes=67_043_328
        ),
        name="exchange",
    )(activations, out_grad, pre, ids, wt, down_weight[0])
    rows_act, rows_grad = rows_act.reshape(slots, width), rows_grad.reshape(slots, width)
    ha, gg, gu = (value.reshape(slots, hidden) for value in (ha, gg, gu))
    grad_gate = contract_rows(rows_act, gg)[None]
    grad_up = contract_rows(rows_act, gu)[None]
    grad_down = contract_rows(ha, rows_grad)[None]
    return (grad_gate, grad_up, grad_down)


def solution(mesh):
    placed = (
        P("gx", "gy"),
        P("gx", "gy"),
        P("gx", None, "gy"),
        P("gx", None, "gy"),
        P("gx", None),
        P("gx", None),
        P("gx", None, "gy"),
    )
    return jax.shard_map(
        on_device,
        mesh=mesh,
        in_specs=placed,
        out_specs=(P("gx", "gy", None), P("gx", "gy", None), P("gx", None, "gy")),
        check_vma=False,
    )
```

```python
import functools

import jax
import jax.numpy as jnp
from jax import lax
from jax.experimental import pallas as pl
from jax.experimental.pallas import tpu as pltpu
from jax.sharding import PartitionSpec as P

MOST = 48
F32 = jnp.float32
BF16 = jnp.bfloat16
MESH = pl.DeviceIdType.MESH


def dot(left, right):
    return jnp.dot(left, right, preferred_element_type=F32)


def exchange_kernel(
    n_gx,
    n_gy,
    top,
    act_ref,
    grad_ref,
    pre_ref,
    ids_ref,
    wt_ref,
    down_hbm,
    rows_act,
    rows_grad,
    ha_ref,
    gg_ref,
    gu_ref,
    down,
    act_send,
    grad_send,
    pre_all,
    pre_send,
    pre_rows,
    part,
    part_in,
    hid,
    down_sem,
    act_ss,
    act_rs,
    grad_ss,
    grad_rs,
    all_ss,
    all_rs,
    pre_ss,
    pre_rs,
    part_ss,
    part_rs,
    hid_ss,
    hid_rs,
):
    me = lax.axis_index("gx")
    my = lax.axis_index("gy")
    tokens = act_ref.shape[0]
    routes = tokens * top
    slots = n_gx * MOST
    per = n_gx // n_gy
    block = per * MOST
    share = pre_ref.shape[1] // 2

    def to_gx(src, dst, ss, rs, other):
        return pltpu.make_async_remote_copy(
            src_ref=src, dst_ref=dst, send_sem=ss, recv_sem=rs,
            device_id={"gx": other}, device_id_type=MESH,
        )

    def to_gy(src, dst, ss, rs, other):
        return pltpu.make_async_remote_copy(
            src_ref=src, dst_ref=dst, send_sem=ss, recv_sem=rs,
            device_id={"gy": other}, device_id_type=MESH,
        )

    def pass_on(src, buf, ss, rs, s, up, down):
        if up:

            @pl.when(my < n_gy - 1)
            def _():
                to_gy(src, buf.at[s], ss.at[s], rs.at[s], my + 1).start()

        if down:

            @pl.when(my > 0)
            def _():
                to_gy(src, buf.at[s], ss.at[n_gy + s], rs.at[s], my - 1).start()

    def hop(buf, ss, rs, h):
        below = jnp.maximum(my - h, 0)
        above = jnp.minimum(my + h, n_gy - 1)

        @pl.when(my >= h)
        def _():
            to_gy(buf.at[below], buf.at[below], ss.at[below], rs.at[below], my).wait_recv()
            pass_on(buf.at[below], buf, ss, rs, below, True, False)

        @pl.when(my + h < n_gy)
        def _():
            to_gy(buf.at[above], buf.at[above], ss.at[above], rs.at[above], my).wait_recv()
            pass_on(buf.at[above], buf, ss, rs, above, False, True)

    def drain(src, buf, ss, rs):
        for s in range(n_gy):

            @pl.when((my >= s) & (my < n_gy - 1))
            def _():
                to_gy(src, buf.at[s], ss.at[s], rs.at[s], my).wait_send()

            @pl.when((my <= s) & (my > 0))
            def _():
                to_gy(src, buf.at[s], ss.at[n_gy + s], rs.at[s], my).wait_send()

    barrier = pltpu.get_barrier_semaphore()
    for d in range(1, n_gx):
        pl.semaphore_signal(
            barrier, inc=1, device_id={"gx": lax.rem(me + d, n_gx)}, device_id_type=MESH
        )
    for d in range(1, n_gy):
        pl.semaphore_signal(
            barrier, inc=1, device_id={"gy": lax.rem(my + d, n_gy)}, device_id_type=MESH
        )
    down_copy = pltpu.make_async_copy(down_hbm, down, down_sem)
    down_copy.start()
    pl.semaphore_wait(barrier, n_gx - 1 + n_gy - 1)

    pass_on(pre_ref, pre_all, all_ss, all_rs, my, True, True)
    pre_all[my] = pre_ref[...]

    ids = ids_ref[...]
    height = max(n_gx, 16)
    expert = lax.broadcasted_iota(jnp.int32, (height, routes), 0)
    named = (expert == ids).astype(F32)
    before = lax.broadcasted_iota(jnp.int32, (tokens, tokens), 0)
    after = lax.broadcasted_iota(jnp.int32, (tokens, tokens), 1)
    less = (before < after).astype(F32).astype(BF16)
    upto = (before <= after).astype(F32).astype(BF16)
    named_low = named.astype(BF16)
    counts = []
    for kb in range(top):
        total = jnp.zeros((height, tokens), F32)
        for ka in range(top):
            total += dot(
                named_low[:, ka * tokens : (ka + 1) * tokens], upto if ka < kb else less
            )
        counts.append(total)
    count = jnp.concatenate(counts, axis=1)
    rank = jnp.sum(count * named, axis=0, keepdims=True)
    slot = ids * MOST + rank.astype(jnp.int32)
    places = lax.broadcasted_iota(jnp.int32, (slots, routes), 0)
    chosen = places == slot
    pick = chosen.astype(F32)
    weight = jnp.sum(pick * wt_ref[...], axis=1, keepdims=True)
    pick_tok = pick[:, :tokens]
    for k in range(1, top):
        pick_tok = pick_tok + pick[:, k * tokens : (k + 1) * tokens]
    pick_tok = pick_tok.astype(BF16)
    pick = pick.astype(BF16)

    width = grad_ref.shape[1]
    grad_send[...] = (
        (dot(pick_tok, grad_ref[...]) * weight).astype(BF16).reshape(n_gx, MOST, width)
    )
    for d in range(1, n_gx):
        other = lax.rem(me + d, n_gx)
        to_gx(
            grad_send.at[other], rows_grad.at[me], grad_ss.at[d], grad_rs.at[me], other
        ).start()
    rows_grad[me] = grad_send[me]

    act_send[...] = dot(pick_tok, act_ref[...]).astype(BF16).reshape(n_gx, MOST, width)
    for d in range(1, n_gx):
        other = lax.rem(me + d, n_gx)
        to_gx(
            act_send.at[other], rows_act.at[me], act_ss.at[d], act_rs.at[me], other
        ).start()
    rows_act[me] = act_send[me]

    down_copy.wait()
    home = me // per
    for i in range(n_gy):
        q = lax.rem(home + n_gy - i, n_gy)
        for j in range(per):
            s = q * per + j

            @pl.when(s != me)
            def _():
                to_gx(
                    grad_send.at[0], rows_grad.at[s], grad_ss.at[0], grad_rs.at[s], me
                ).wait_recv()

        rows = rows_grad[pl.ds(q * per, per)].reshape(block, width)
        value = lax.dot_general(
            rows, down[...], (((1,), (1,)), ((), ())), preferred_element_type=F32
        ).astype(BF16)
        part[q] = value

        @pl.when(q != my)
        def _():
            to_gy(part.at[q], part_in.at[my], part_ss.at[q], part_rs.at[my], q).start()

        @pl.when(q == my)
        def _():
            part_in[my] = part[q]

        if i + 1 < n_gy - 1:
            hop(pre_all, all_ss, all_rs, i + 1)

    if n_gy > 1:
        hop(pre_all, all_ss, all_rs, n_gy - 1)
    for y in range(n_gy):
        pre_send[:, y] = (
            dot(pick, pre_all[y]).astype(BF16).reshape(n_gx, MOST, 2 * share)
        )
    for d in range(1, n_gx):
        other = lax.rem(me + d, n_gx)
        to_gx(
            pre_send.at[other], pre_rows.at[me], pre_ss.at[d], pre_rs.at[me], other
        ).start()
    pre_rows[me] = pre_send[me]

    for d in range(1, n_gy):
        other = lax.rem(my + d, n_gy)
        to_gy(part.at[0], part_in.at[other], part_ss.at[0], part_rs.at[other], my).wait_recv()
    total = part_in[0].astype(F32)
    for y in range(1, n_gy):
        total = total + part_in[y].astype(F32)
    hid[my] = total.astype(BF16)
    pass_on(hid.at[my], hid, hid_ss, hid_rs, my, True, True)
    for h in range(1, n_gy):
        hop(hid, hid_ss, hid_rs, h)

    for d in range(1, n_gx):
        other = lax.rem(me + d, n_gx)
        to_gx(pre_send.at[0], pre_rows.at[other], pre_ss.at[0], pre_rs.at[other], me).wait_recv()

    @pl.loop(0, n_gy)
    def _(q):
        for y in range(n_gy):
            both = pre_rows[pl.ds(q * per, per), y].reshape(block, 2 * share).astype(F32)
            gate, up = both[:, :share], both[:, share:]
            sig = jax.nn.sigmoid(gate)
            silu = gate * sig
            cols = slice(y * share, (y + 1) * share)
            value = hid[q, :, cols].astype(F32)
            ha_ref[q, :, cols] = (silu * up).astype(BF16)
            gg_ref[q, :, cols] = (value * up * sig * (1.0 + gate * (1.0 - sig))).astype(BF16)
            gu_ref[q, :, cols] = (value * silu).astype(BF16)

    for d in range(1, n_gx):
        other = lax.rem(me + d, n_gx)
        to_gx(act_send.at[0], rows_act.at[other], act_ss.at[0], act_rs.at[other], me).wait_recv()
    for d in range(1, n_gx):
        other = lax.rem(me + d, n_gx)
        for src, dst, ss, rs in (
            (grad_send, rows_grad, grad_ss, grad_rs),
            (act_send, rows_act, act_ss, act_rs),
            (pre_send, pre_rows, pre_ss, pre_rs),
        ):
            to_gx(src.at[other], dst.at[me], ss.at[d], rs.at[me], other).wait_send()
    for d in range(1, n_gy):
        other = lax.rem(my + d, n_gy)
        to_gy(part.at[other], part_in.at[my], part_ss.at[other], part_rs.at[my], other).wait_send()
    drain(pre_ref, pre_all, all_ss, all_rs)
    drain(hid.at[0], hid, hid_ss, hid_rs)


def product_kernel(act_ref, grad_ref, ha_ref, gg_ref, gu_ref, gate_ref, up_ref, down_ref, turned):
    @pl.when(pl.program_id(0) == 0)
    def _():
        turned[...] = ha_ref[...].T

    act = act_ref[...].T
    gate_ref[...] = dot(act, gg_ref[...]).astype(BF16)
    up_ref[...] = dot(act, gu_ref[...]).astype(BF16)
    down_ref[...] = dot(turned[...], grad_ref[...]).astype(BF16)


def products(rows_act, rows_grad, ha, gg, gu):
    slots, width = rows_act.shape
    hidden = ha.shape[1]
    tile = 256 if width % 256 == 0 else width
    wide = pl.BlockSpec((slots, tile), lambda i: (0, i))
    whole = pl.BlockSpec((slots, hidden), lambda i: (0, 0), pipeline_mode=pl.Buffered(1))
    tall = pl.BlockSpec((None, tile, hidden), lambda i: (0, i, 0))
    flat = pl.BlockSpec((None, hidden, tile), lambda i: (0, 0, i))
    return pl.pallas_call(
        product_kernel,
        grid=(width // tile,),
        out_shape=(
            jax.ShapeDtypeStruct((1, width, hidden), BF16),
            jax.ShapeDtypeStruct((1, width, hidden), BF16),
            jax.ShapeDtypeStruct((1, hidden, width), BF16),
        ),
        in_specs=[wide, wide, whole, whole, whole],
        out_specs=(tall, tall, flat),
        scratch_shapes=[pltpu.VMEM((hidden, slots), BF16)],
        compiler_params=pltpu.CompilerParams(
            dimension_semantics=("arbitrary",), vmem_limit_bytes=40 * 1024 * 1024
        ),
        name="products",
    )(rows_act, rows_grad, ha, gg, gu)


def on_device(activations, out_grad, saved_gate, saved_up, route_ids, route_weight, down_weight):
    n_gx, n_gy = lax.axis_size("gx"), lax.axis_size("gy")
    tokens, top = route_ids.shape
    routes, slots = tokens * top, n_gx * MOST
    width, share = activations.shape[1], saved_gate.shape[2]
    hidden = down_weight.shape[1]
    rows = slots // n_gy
    ids = route_ids.T.reshape(1, routes)
    wt = route_weight.T.reshape(1, routes)
    pre = jnp.concatenate([saved_gate, saved_up], axis=2)
    pre = pre.transpose(1, 0, 2).reshape(routes, 2 * share)
    vmem = pl.BlockSpec(memory_space=pltpu.VMEM)
    dma = pltpu.SemaphoreType.DMA
    shape = jax.ShapeDtypeStruct
    rows_act, rows_grad, ha, gg, gu = pl.pallas_call(
        functools.partial(exchange_kernel, n_gx, n_gy, top),
        out_shape=(
            shape((n_gx, MOST, width), BF16),
            shape((n_gx, MOST, width), BF16),
            shape((n_gy, rows, hidden), BF16),
            shape((n_gy, rows, hidden), BF16),
            shape((n_gy, rows, hidden), BF16),
        ),
        in_specs=[vmem] * 5 + [pl.BlockSpec(memory_space=pl.ANY)],
        out_specs=[vmem] * 5,
        scratch_shapes=[
            pltpu.VMEM((hidden, width), BF16),
            pltpu.VMEM((n_gx, MOST, width), BF16),
            pltpu.VMEM((n_gx, MOST, width), BF16),
            pltpu.VMEM((n_gy, routes, 2 * share), BF16),
            pltpu.VMEM((n_gx, n_gy, MOST, 2 * share), BF16),
            pltpu.VMEM((n_gx, n_gy, MOST, 2 * share), BF16),
            pltpu.VMEM((n_gy, rows, hidden), BF16),
            pltpu.VMEM((n_gy, rows, hidden), BF16),
            pltpu.VMEM((n_gy, rows, hidden), BF16),
            dma,
            dma((n_gx,)), dma((n_gx,)), dma((n_gx,)), dma((n_gx,)),
            dma((2 * n_gy,)), dma((n_gy,)),
            dma((n_gx,)), dma((n_gx,)),
            dma((n_gy,)), dma((n_gy,)), dma((2 * n_gy,)), dma((n_gy,)),
        ],
        compiler_params=pltpu.CompilerParams(
            collective_id=0, has_side_effects=True, vmem_limit_bytes=67_043_328
        ),
        name="exchange",
    )(activations, out_grad, pre, ids, wt, down_weight[0])
    rows_act, rows_grad = rows_act.reshape(slots, width), rows_grad.reshape(slots, width)
    ha, gg, gu = (value.reshape(slots, hidden) for value in (ha, gg, gu))
    return tuple(products(rows_act, rows_grad, ha, gg, gu))


def solution(mesh):
    placed = (
        P("gx", "gy"),
        P("gx", "gy"),
        P("gx", None, "gy"),
        P("gx", None, "gy"),
        P("gx", None),
        P("gx", None),
        P("gx", None, "gy"),
    )
    return jax.shard_map(
        on_device,
        mesh=mesh,
        in_specs=placed,
        out_specs=(P("gx", "gy", None), P("gx", "gy", None), P("gx", None, "gy")),
        check_vma=False,
    )
```

```python
import functools

import jax
import jax.numpy as jnp
from jax import lax
from jax.experimental import pallas as pl
from jax.experimental.pallas import tpu as pltpu
from jax.sharding import PartitionSpec as P

MOST = 48
F32 = jnp.float32
BF16 = jnp.bfloat16
MESH = pl.DeviceIdType.MESH


def dot(left, right):
    return jnp.dot(left, right, preferred_element_type=F32)


def exchange_kernel(
    n_gx,
    n_gy,
    top,
    act_ref,
    grad_ref,
    pre_ref,
    ids_ref,
    wt_ref,
    down_hbm,
    rows_act,
    rows_grad,
    ha_ref,
    gg_ref,
    gu_ref,
    down,
    act_send,
    grad_send,
    pre_all,
    pre_send,
    pre_rows,
    part,
    part_in,
    hid,
    down_sem,
    act_ss,
    act_rs,
    grad_ss,
    grad_rs,
    all_ss,
    all_rs,
    pre_ss,
    pre_rs,
    part_ss,
    part_rs,
    hid_ss,
    hid_rs,
):
    me = lax.axis_index("gx")
    my = lax.axis_index("gy")
    tokens = act_ref.shape[0]
    routes = tokens * top
    slots = n_gx * MOST
    per = n_gx // n_gy
    block = per * MOST
    share = pre_ref.shape[1] // 2

    def to_gx(src, dst, ss, rs, other):
        return pltpu.make_async_remote_copy(
            src_ref=src, dst_ref=dst, send_sem=ss, recv_sem=rs,
            device_id={"gx": other}, device_id_type=MESH,
        )

    def to_gy(src, dst, ss, rs, other):
        return pltpu.make_async_remote_copy(
            src_ref=src, dst_ref=dst, send_sem=ss, recv_sem=rs,
            device_id={"gy": other}, device_id_type=MESH,
        )

    def pass_on(src, buf, ss, rs, s, up, down):
        if up:

            @pl.when(my < n_gy - 1)
            def _():
                to_gy(src, buf.at[s], ss.at[s], rs.at[s], my + 1).start()

        if down:

            @pl.when(my > 0)
            def _():
                to_gy(src, buf.at[s], ss.at[n_gy + s], rs.at[s], my - 1).start()

    def hop(buf, ss, rs, h):
        below = jnp.maximum(my - h, 0)
        above = jnp.minimum(my + h, n_gy - 1)

        @pl.when(my >= h)
        def _():
            to_gy(buf.at[below], buf.at[below], ss.at[below], rs.at[below], my).wait_recv()
            pass_on(buf.at[below], buf, ss, rs, below, True, False)

        @pl.when(my + h < n_gy)
        def _():
            to_gy(buf.at[above], buf.at[above], ss.at[above], rs.at[above], my).wait_recv()
            pass_on(buf.at[above], buf, ss, rs, above, False, True)

    def drain(src, buf, ss, rs):
        for s in range(n_gy):

            @pl.when((my >= s) & (my < n_gy - 1))
            def _():
                to_gy(src, buf.at[s], ss.at[s], rs.at[s], my).wait_send()

            @pl.when((my <= s) & (my > 0))
            def _():
                to_gy(src, buf.at[s], ss.at[n_gy + s], rs.at[s], my).wait_send()

    barrier = pltpu.get_barrier_semaphore()
    for d in range(1, n_gx):
        pl.semaphore_signal(
            barrier, inc=1, device_id={"gx": lax.rem(me + d, n_gx)}, device_id_type=MESH
        )
    for d in range(1, n_gy):
        pl.semaphore_signal(
            barrier, inc=1, device_id={"gy": lax.rem(my + d, n_gy)}, device_id_type=MESH
        )
    down_copy = pltpu.make_async_copy(down_hbm, down, down_sem)
    down_copy.start()
    pl.semaphore_wait(barrier, n_gx - 1 + n_gy - 1)

    pass_on(pre_ref, pre_all, all_ss, all_rs, my, True, True)
    pre_all[my] = pre_ref[...]

    ids = ids_ref[...]
    height = max(n_gx, 16)
    expert = lax.broadcasted_iota(jnp.int32, (height, routes), 0)
    named = (expert == ids).astype(F32)
    before = lax.broadcasted_iota(jnp.int32, (tokens, tokens), 0)
    after = lax.broadcasted_iota(jnp.int32, (tokens, tokens), 1)
    less = (before < after).astype(F32).astype(BF16)
    upto = (before <= after).astype(F32).astype(BF16)
    named_low = named.astype(BF16)
    counts = []
    for kb in range(top):
        total = jnp.zeros((height, tokens), F32)
        for ka in range(top):
            total += dot(
                named_low[:, ka * tokens : (ka + 1) * tokens], upto if ka < kb else less
            )
        counts.append(total)
    count = jnp.concatenate(counts, axis=1)
    rank = jnp.sum(count * named, axis=0, keepdims=True)
    slot = ids * MOST + rank.astype(jnp.int32)
    places = lax.broadcasted_iota(jnp.int32, (slots, routes), 0)
    chosen = places == slot
    pick = chosen.astype(F32)
    weight = jnp.sum(pick * wt_ref[...], axis=1, keepdims=True)
    pick_tok = pick[:, :tokens]
    for k in range(1, top):
        pick_tok = pick_tok + pick[:, k * tokens : (k + 1) * tokens]
    pick_tok = pick_tok.astype(BF16)
    pick = pick.astype(BF16)

    width = grad_ref.shape[1]
    grad_send[...] = (
        (dot(pick_tok, grad_ref[...]) * weight).astype(BF16).reshape(n_gx, MOST, width)
    )
    for d in range(1, n_gx):
        other = lax.rem(me + d, n_gx)
        to_gx(
            grad_send.at[other], rows_grad.at[me], grad_ss.at[d], grad_rs.at[me], other
        ).start()
    rows_grad[me] = grad_send[me]

    act_send[...] = dot(pick_tok, act_ref[...]).astype(BF16).reshape(n_gx, MOST, width)
    for d in range(1, n_gx):
        other = lax.rem(me + d, n_gx)
        to_gx(
            act_send.at[other], rows_act.at[me], act_ss.at[d], act_rs.at[me], other
        ).start()
    rows_act[me] = act_send[me]

    down_copy.wait()
    home = me // per
    for i in range(n_gy):
        q = lax.rem(home + n_gy - i, n_gy)
        for j in range(per):
            s = q * per + j

            @pl.when(s != me)
            def _():
                to_gx(
                    grad_send.at[0], rows_grad.at[s], grad_ss.at[0], grad_rs.at[s], me
                ).wait_recv()

        rows = rows_grad[pl.ds(q * per, per)].reshape(block, width)
        value = lax.dot_general(
            rows, down[...], (((1,), (1,)), ((), ())), preferred_element_type=F32
        ).astype(BF16)
        part[q] = value

        @pl.when(q != my)
        def _():
            to_gy(part.at[q], part_in.at[my], part_ss.at[q], part_rs.at[my], q).start()

        @pl.when(q == my)
        def _():
            part_in[my] = part[q]

        if i + 1 < n_gy - 1:
            hop(pre_all, all_ss, all_rs, i + 1)

    if n_gy > 1:
        hop(pre_all, all_ss, all_rs, n_gy - 1)
    for y in range(n_gy):
        pre_send[:, y] = (
            dot(pick, pre_all[y]).astype(BF16).reshape(n_gx, MOST, 2 * share)
        )
    for d in range(1, n_gx):
        other = lax.rem(me + d, n_gx)
        to_gx(
            pre_send.at[other], pre_rows.at[me], pre_ss.at[d], pre_rs.at[me], other
        ).start()
    pre_rows[me] = pre_send[me]

    for d in range(1, n_gy):
        other = lax.rem(my + d, n_gy)
        to_gy(part.at[0], part_in.at[other], part_ss.at[0], part_rs.at[other], my).wait_recv()
    total = part_in[0].astype(F32)
    for y in range(1, n_gy):
        total = total + part_in[y].astype(F32)
    hid[my] = total.astype(BF16)
    pass_on(hid.at[my], hid, hid_ss, hid_rs, my, True, True)
    for h in range(1, n_gy):
        hop(hid, hid_ss, hid_rs, h)

    for d in range(1, n_gx):
        other = lax.rem(me + d, n_gx)
        to_gx(pre_send.at[0], pre_rows.at[other], pre_ss.at[0], pre_rs.at[other], me).wait_recv()

    @pl.loop(0, n_gy)
    def _(q):
        for y in range(n_gy):
            both = pre_rows[pl.ds(q * per, per), y].reshape(block, 2 * share).astype(F32)
            gate, up = both[:, :share], both[:, share:]
            sig = jax.nn.sigmoid(gate)
            silu = gate * sig
            cols = slice(y * share, (y + 1) * share)
            value = hid[q, :, cols].astype(F32)
            ha_ref[q, :, cols] = (silu * up).astype(BF16)
            gg_ref[q, :, cols] = (value * up * sig * (1.0 + gate * (1.0 - sig))).astype(BF16)
            gu_ref[q, :, cols] = (value * silu).astype(BF16)

    for d in range(1, n_gx):
        other = lax.rem(me + d, n_gx)
        to_gx(act_send.at[0], rows_act.at[other], act_ss.at[0], act_rs.at[other], me).wait_recv()
    for d in range(1, n_gx):
        other = lax.rem(me + d, n_gx)
        for src, dst, ss, rs in (
            (grad_send, rows_grad, grad_ss, grad_rs),
            (act_send, rows_act, act_ss, act_rs),
            (pre_send, pre_rows, pre_ss, pre_rs),
        ):
            to_gx(src.at[other], dst.at[me], ss.at[d], rs.at[me], other).wait_send()
    for d in range(1, n_gy):
        other = lax.rem(my + d, n_gy)
        to_gy(part.at[other], part_in.at[my], part_ss.at[other], part_rs.at[my], other).wait_send()
    drain(pre_ref, pre_all, all_ss, all_rs)
    drain(hid.at[0], hid, hid_ss, hid_rs)


def product_kernel(act_ref, grad_ref, ha_ref, gg_ref, gu_ref, gate_ref, up_ref, down_ref, turned):
    @pl.when(pl.program_id(0) == 0)
    def _():
        turned[...] = ha_ref[...].T

    act = act_ref[...].T
    gate_ref[...] = dot(act, gg_ref[...]).astype(BF16)
    up_ref[...] = dot(act, gu_ref[...]).astype(BF16)
    down_ref[...] = dot(turned[...], grad_ref[...]).astype(BF16)


def products(rows_act, rows_grad, ha, gg, gu):
    slots, width = rows_act.shape
    hidden = ha.shape[1]
    tile = 256 if width % 256 == 0 else width
    wide = pl.BlockSpec((slots, tile), lambda i: (0, i))
    whole = pl.BlockSpec((slots, hidden), lambda i: (0, 0), pipeline_mode=pl.Buffered(1))
    tall = pl.BlockSpec((None, tile, hidden), lambda i: (0, i, 0))
    flat = pl.BlockSpec((None, hidden, tile), lambda i: (0, 0, i))
    return pl.pallas_call(
        product_kernel,
        grid=(width // tile,),
        out_shape=(
            jax.ShapeDtypeStruct((1, width, hidden), BF16),
            jax.ShapeDtypeStruct((1, width, hidden), BF16),
            jax.ShapeDtypeStruct((1, hidden, width), BF16),
        ),
        in_specs=[wide, wide, whole, whole, whole],
        out_specs=(tall, tall, flat),
        scratch_shapes=[pltpu.VMEM((hidden, slots), BF16)],
        compiler_params=pltpu.CompilerParams(
            dimension_semantics=("arbitrary",), vmem_limit_bytes=67_043_328
        ),
        name="products",
    )(rows_act, rows_grad, ha, gg, gu)


def on_device(activations, out_grad, saved_gate, saved_up, route_ids, route_weight, down_weight):
    n_gx, n_gy = lax.axis_size("gx"), lax.axis_size("gy")
    tokens, top = route_ids.shape
    routes, slots = tokens * top, n_gx * MOST
    width, share = activations.shape[1], saved_gate.shape[2]
    hidden = down_weight.shape[1]
    rows = slots // n_gy
    ids = route_ids.T.reshape(1, routes)
    wt = route_weight.T.reshape(1, routes)
    pre = jnp.concatenate([saved_gate, saved_up], axis=2)
    pre = pre.transpose(1, 0, 2).reshape(routes, 2 * share)
    vmem = pl.BlockSpec(memory_space=pltpu.VMEM)
    dma = pltpu.SemaphoreType.DMA
    shape = jax.ShapeDtypeStruct
    rows_act, rows_grad, ha, gg, gu = pl.pallas_call(
        functools.partial(exchange_kernel, n_gx, n_gy, top),
        out_shape=(
            shape((n_gx, MOST, width), BF16),
            shape((n_gx, MOST, width), BF16),
            shape((n_gy, rows, hidden), BF16),
            shape((n_gy, rows, hidden), BF16),
            shape((n_gy, rows, hidden), BF16),
        ),
        in_specs=[vmem] * 5 + [pl.BlockSpec(memory_space=pl.ANY)],
        out_specs=[vmem] * 5,
        scratch_shapes=[
            pltpu.VMEM((hidden, width), BF16),
            pltpu.VMEM((n_gx, MOST, width), BF16),
            pltpu.VMEM((n_gx, MOST, width), BF16),
            pltpu.VMEM((n_gy, routes, 2 * share), BF16),
            pltpu.VMEM((n_gx, n_gy, MOST, 2 * share), BF16),
            pltpu.VMEM((n_gx, n_gy, MOST, 2 * share), BF16),
            pltpu.VMEM((n_gy, rows, hidden), BF16),
            pltpu.VMEM((n_gy, rows, hidden), BF16),
            pltpu.VMEM((n_gy, rows, hidden), BF16),
            dma,
            dma((n_gx,)), dma((n_gx,)), dma((n_gx,)), dma((n_gx,)),
            dma((2 * n_gy,)), dma((n_gy,)),
            dma((n_gx,)), dma((n_gx,)),
            dma((n_gy,)), dma((n_gy,)), dma((2 * n_gy,)), dma((n_gy,)),
        ],
        compiler_params=pltpu.CompilerParams(
            collective_id=0, has_side_effects=True, vmem_limit_bytes=67_043_328
        ),
        name="exchange",
    )(activations, out_grad, pre, ids, wt, down_weight[0])
    rows_act, rows_grad = rows_act.reshape(slots, width), rows_grad.reshape(slots, width)
    ha, gg, gu = (value.reshape(slots, hidden) for value in (ha, gg, gu))
    return tuple(products(rows_act, rows_grad, ha, gg, gu))


def solution(mesh):
    placed = (
        P("gx", "gy"),
        P("gx", "gy"),
        P("gx", None, "gy"),
        P("gx", None, "gy"),
        P("gx", None),
        P("gx", None),
        P("gx", None, "gy"),
    )
    return jax.shard_map(
        on_device,
        mesh=mesh,
        in_specs=placed,
        out_specs=(P("gx", "gy", None), P("gx", "gy", None), P("gx", None, "gy")),
        check_vma=False,
    )
```
